256 devices in a mesh: dp: 4 (over x), expert: 64 (over z, y, core).
Axes of the slice: x: 4, y: 4, z: 8, core: 2. Of those that a mesh axis runs over, the one named last changes fastest.
Arguments:
- tokens: bfloat16 [32768, 1024], P(('dp', 'expert')), may hold values from -6 to 6
- routes: int32 [32768, 8], P(('dp', 'expert')), may hold values from 0 to 127, all different within a row; in each aligned block of 128 rows (0 to 127, 128 to 255, ...) at most 12 rows name the same one
- gates: float32 [32768, 8], P(('dp', 'expert')), may hold values from 0.05 to 0.5
- cotangent: bfloat16 [32768, 1024], P(('dp', 'expert')), may hold values from -6 to 6
- partner: int32 [128], replicated, may hold values from 0 to 127, as said below
- w_gate_up: bfloat16 [128, 1024, 768], P('expert'), may hold values from -0.1875 to 0.1875
- w_down: bfloat16 [128, 1024, 384], P('expert'), may hold values from -0.3125 to 0.3125
Outputs:
- mixed: bfloat16 [32768, 1024], P(('dp', 'expert'))
- grad_tokens: bfloat16 [32768, 1024], P(('dp', 'expert'))
- grad_gate_up: float32 [128, 1024, 768], P('expert', 'dp')
- grad_down: float32 [128, 1024, 384], P('expert', 'dp')
The draws below stay inside these ranges and needn't reach their ends.
Inputs may be any that keep to these rules, and one draw needn't show every extreme that they name: `routes`: A token names 8 different experts. In each device's block of 128 consecutive tokens no expert is named by more than 12 tokens, a bound that some block reaches. partner is a permutation that is its own inverse: each slot either keeps its expert or trades it with one slot of the device half the expert axis away (slot s lies on index s // 2 of the expert axis); each device trades at most one of its slots, and some slots trade in every draw.
All inputs are finite; a program needn't handle non-finite values.
Results may differ from the reference program's by a relative error of at most 0.01.
Values may be sent and summed in bfloat16 or wider, within the bound.
A program may use at most 128 MiB of HBM per device.

```python
import math
import jax
import jax.numpy as jnp
import numpy as np
from jax import lax

D = 1024
FF = 384
TOP = 8
EXP_DEV = 2
TOK_DEV = 128
EXPERTS = 128
CAP = 12
TOKENS = 32768
N_DP = 4
N_EXPERT = 64


def draw_partner(key, part):
    half_dev = EXPERTS // (2 * EXP_DEV)
    key_flag = jax.random.fold_in(key, 11)
    key_low = jax.random.fold_in(key, 12)
    key_high = jax.random.fold_in(key, 13)
    flags = jax.random.randint(key_flag, (half_dev,), 0, 2, dtype=jnp.int32)
    flags = flags.at[0].set(1)
    low_pick = jax.random.randint(key_low, (half_dev,), 0, EXP_DEV, dtype=jnp.int32)
    high_pick = jax.random.randint(key_high, (half_dev,), 0, EXP_DEV, dtype=jnp.int32)
    devices = jnp.arange(half_dev, dtype=jnp.int32)
    low_slot = devices * EXP_DEV + low_pick
    high_slot = (devices + half_dev) * EXP_DEV + high_pick
    result = jnp.arange(EXPERTS, dtype=jnp.int32)
    result = result.at[low_slot].set(jnp.where(flags == 1, high_slot, low_slot))
    result = result.at[high_slot].set(jnp.where(flags == 1, low_slot, high_slot))
    return result


def block_scale(key, dims, split, smallest, high):
    factor_of = 1.0
    for dim, parts in split:
        heights = jax.random.uniform(jax.random.fold_in(jax.random.fold_in(key, 6), dim), (parts,), jnp.float32, smallest / len(split), high / len(split))
        factor_of = factor_of * jnp.repeat(jnp.exp(heights), dims[dim] // parts).reshape((-1,) + (1,) * (len(dims) - 1 - dim))
    return factor_of


def shared_out(rng, own, number, rows, amount, top, reach, skew):
    sequence = jax.random.permutation(rng, amount)
    heavy_load, ordinary = portions_of(amount, rows * top, reach, skew, True), portions_of(amount, rows * top, reach, skew, False)
    places = jnp.arange(amount)

    def named(tallies, turn):
        used = int((tallies > 0).sum())
        fixed = max(1, used // 4)
        passed = fixed + (places - fixed + turn * (used - fixed)) % max(1, amount - fixed)
        return jnp.zeros((amount,), jnp.int32).at[sequence[jnp.where(places < fixed, places, passed)]].set(jnp.asarray(tallies, jnp.int32))

    tallies = jnp.where(number % 4 == 0, named(heavy_load, number // 4), named(ordinary, number - number // 4 - 1))
    mixed = jax.random.permutation(jax.random.fold_in(own, 3), amount)
    giver, taker = mixed[0:amount // 2 * 2:2], mixed[1:amount // 2 * 2:2]
    slack = jnp.minimum(tallies[giver] - 1, reach - tallies[taker]) // 2
    slack = jnp.where((giver == sequence[0]) | (taker == sequence[0]) | (tallies[taker] == 0), 0, jnp.maximum(slack, 0))
    passed = jax.random.randint(jax.random.fold_in(own, 4), (amount // 2,), 0, 1 << 20) % (slack + 1)
    tallies = tallies.at[giver].add(-passed).at[taker].add(passed)
    labels = jnp.searchsorted(jnp.cumsum(tallies), jnp.arange(rows * top), side="right").astype(jnp.int32)
    listing = labels.reshape(top, rows).T
    listing = listing[jax.random.permutation(jax.random.fold_in(own, 1), rows)]
    turn = jax.random.randint(jax.random.fold_in(own, 2), (rows, 1), 0, top)
    return jnp.take_along_axis(listing, (jnp.arange(top)[None, :] + turn) % top, axis=1)


def portions_of(number_of, total, bound, skew, full):
    weights = [(1 << 20) // math.isqrt(rank ** skew) + 1 for rank in range(1, number_of + 1)]
    largest = bound if full else min(bound, max(-(-total // number_of), total * weights[0] // sum(weights)))
    least = 1 if total - largest >= number_of - 1 else 0
    given, surplus = [largest] + [least] * (number_of - 1), total - largest - least * (number_of - 1)
    while surplus > 0:
        free = [i for i in range(1, number_of) if given[i] < largest] or [i for i in range(1, number_of) if given[i] < bound]
        mass, budget = sum([weights[i] for i in free]), surplus
        for i in free:
            addition = min(bound - given[i], max(1, budget * weights[i] // mass), surplus)
            given[i] = given[i] + addition
            surplus = surplus - addition
    return np.array(given)


def normal_values(own_key, extent, spread, limit, shards=(), kind=jnp.bfloat16):
    values = jax.random.normal(own_key, extent, jnp.float32) * spread
    if len(shards) > 0:
        values = block_scale(own_key, extent, shards, -0.22, 0.18) * values
    return jnp.clip(values, min=-limit, max=limit).astype(kind)


def setup_inputs(seed: int = 0) -> dict:
    seeds = jax.random.split(jax.random.key(seed), 8)
    tokens = normal_values(seeds[0], (TOKENS, D), 1.0, 6.0, ((0, 256),))
    routes_keys = jax.random.split(jax.random.fold_in(seeds[1], 1), TOKENS // TOK_DEV)
    routes_turns = jax.random.permutation(jax.random.fold_in(seeds[1], 3), TOKENS // TOK_DEV)
    routes = jax.vmap(lambda own, number: shared_out(jax.random.fold_in(seeds[1], 2), own, number, TOK_DEV, EXPERTS, TOP, CAP, 2))(routes_keys, routes_turns).reshape((TOKENS, TOP))
    gates = jnp.clip(0.05 + 0.45 * jax.random.uniform(seeds[2], (TOKENS, TOP), jnp.float32) ** block_scale(seeds[2], (TOKENS, TOP), ((0, 256),), -0.2, 0.2), 0.05, 0.5)
    cotangent = normal_values(seeds[3], (TOKENS, D), 1.0, 6.0, ((0, 256),))
    partner = draw_partner(jax.random.fold_in(seeds[7], 71), 0)
    w_gate_up = normal_values(seeds[5], (EXPERTS, D, 2 * FF), D ** -0.5, 0.1875, ((0, 64),))
    w_down = normal_values(seeds[6], (EXPERTS, D, FF), FF ** -0.5, 0.3125, ((0, 64),))
    return {"tokens": tokens, "routes": routes, "gates": gates, "cotangent": cotangent, "partner": partner, "w_gate_up": w_gate_up, "w_down": w_down}


grad_scale = 0.0625


def reference(tokens, routes, gates, cotangent, partner, w_gate_up, w_down):
    assign_total = TOKENS * TOP
    most_rows = N_DP * N_EXPERT * CAP
    flat = routes.reshape(-1).astype(jnp.int32)
    order = jnp.argsort(flat, stable=True).astype(jnp.int32)
    sorted_keys = flat[order]
    counts = jnp.zeros((EXPERTS,), jnp.int32).at[flat].add(1)
    starts = (jnp.cumsum(counts) - counts).astype(jnp.int32)
    ranked = jnp.arange(assign_total, dtype=jnp.int32) - starts[sorted_keys]
    table = jnp.full((EXPERTS, most_rows), assign_total, jnp.int32).at[sorted_keys, ranked].set(order)
    token_pad = jnp.concatenate([tokens, jnp.zeros((1, D), tokens.dtype)], axis=0)
    cot_pad = jnp.concatenate([cotangent, jnp.zeros((1, D), cotangent.dtype)], axis=0)
    gate_pad = jnp.concatenate([gates.reshape(-1), jnp.zeros((1,), gates.dtype)], axis=0)
    highest = lax.Precision.HIGHEST

    def one_expert(carry, inputs):
        mixed_sum, grad_sum = carry
        index, weight_gu, weight_dn = inputs
        token_index = (index // TOP).astype(jnp.int32)
        rows = token_pad[token_index].astype(jnp.float32)
        gate_rows = gate_pad[index].astype(jnp.float32)
        wgu_full = weight_gu.astype(jnp.float32)
        wdn_full = weight_dn.astype(jnp.float32)
        pre_act = jnp.dot(rows, wgu_full, preferred_element_type=jnp.float32, precision=highest)
        gate_pre = pre_act[:, :FF]
        up_pre = pre_act[:, FF:]
        sigmoid_gate = jax.nn.sigmoid(gate_pre)
        silu_gate = gate_pre * sigmoid_gate
        hidden = (silu_gate * up_pre).astype(jnp.bfloat16)
        expert_out = jnp.dot(hidden.astype(jnp.float32), wdn_full.T, preferred_element_type=jnp.float32, precision=highest).astype(jnp.bfloat16)
        mixed_sum = mixed_sum.at[token_index].add(gate_rows[:, None] * expert_out.astype(jnp.float32))
        grad_out = (gate_rows[:, None] * cot_pad[token_index].astype(jnp.float32)).astype(jnp.bfloat16)
        grad_out_full = grad_out.astype(jnp.float32)
        grad_hidden = jnp.dot(grad_out_full, wdn_full, preferred_element_type=jnp.float32, precision=highest)
        grad_down = jnp.dot(grad_out_full.T, hidden.astype(jnp.float32), preferred_element_type=jnp.float32, precision=highest)
        grad_gate = grad_hidden * up_pre * sigmoid_gate * (1.0 + gate_pre * (1.0 - sigmoid_gate))
        grad_up = grad_hidden * silu_gate
        grad_pre = jnp.concatenate([grad_gate, grad_up], axis=-1).astype(jnp.bfloat16)
        grad_pre_full = grad_pre.astype(jnp.float32)
        grad_rows = jnp.dot(grad_pre_full, wgu_full.T, preferred_element_type=jnp.float32, precision=highest).astype(jnp.bfloat16)
        grad_sum = grad_sum.at[token_index].add(grad_rows.astype(jnp.float32))
        grad_gu = jnp.dot(rows.T, grad_pre_full, preferred_element_type=jnp.float32, precision=highest)
        stacked = jnp.concatenate([grad_gu, grad_down], axis=-1) * grad_scale
        return (mixed_sum, grad_sum), stacked

    start = (jnp.zeros((TOKENS + 1, D), jnp.float32), jnp.zeros((TOKENS + 1, D), jnp.float32))
    (mixed_sum, grad_sum), expert_grad = lax.scan(one_expert, start, (table, w_gate_up, w_down))
    mixed = mixed_sum[:TOKENS].astype(jnp.bfloat16)
    grad_tokens = grad_sum[:TOKENS].astype(jnp.bfloat16)
    by_slot = jnp.take(expert_grad, partner.astype(jnp.int32), axis=0)
    return mixed, grad_tokens, by_slot[:, :, :2 * FF], by_slot[:, :, 2 * FF:]
```

```python
import functools

import jax
import jax.numpy as jnp
import numpy as np
from jax import lax
from jax.experimental import pallas as pl
from jax.experimental.pallas import tpu as pltpu
from jax.sharding import PartitionSpec as P

MESH = pl.DeviceIdType.MESH
bf16, f32 = jnp.bfloat16, jnp.float32

grad_scale = 0.0625
PLANE = 8
CAP = 12
BLOCKS = 4
ROWS = CAP * BLOCKS
GROUPS = ((0, 1, -1, -2), (2, 3, -3, 4))
PLACE = {offset: (g, b) for g, group in enumerate(GROUPS) for b, offset in enumerate(group)}


def dot_nn(a, b):
    return lax.dot_general(a, b, (((1,), (0,)), ((), ())), preferred_element_type=f32)


def dot_nt(a, b):
    return lax.dot_general(a, b, (((1,), (1,)), ((), ())), preferred_element_type=f32)


def dot_tn(a, b):
    return lax.dot_general(a, b, (((0,), (0,)), ((), ())), preferred_element_type=f32)


def places():
    dp, index = lax.axis_index("dp"), lax.axis_index("expert")
    n_dp, n_z = lax.axis_size("dp"), lax.axis_size("expert") // PLANE
    return dp, index // PLANE, index % PLANE, n_dp, n_z


def remote(src, dst, send, recv, device):
    return pltpu.make_async_remote_copy(
        src_ref=src, dst_ref=dst, send_sem=send, recv_sem=recv, device_id=device, device_id_type=MESH
    )


def greet(devices):
    barrier = pltpu.get_barrier_semaphore()
    for device in devices:
        pl.semaphore_signal(barrier, inc=1, device_id=device, device_id_type=MESH)
    pl.semaphore_wait(barrier, len(devices))


def dispatch_kernel(
    tokens, cot, routes_t, gates_t, partner, expand, wanted, ws_gu, ws_dn,
    got_t, got_c, pick, pick_gate, wr_gu, wr_dn,
    xt, xc, rg, out_t, out_c,
    t_send, t_recv, c_send, c_recv, r_send, r_recv, y_send, y_recv, l_sem, w_send, w_recv, x_send, x_recv,
):
    dp, z, yc, n_dp, n_z = places()

    def at_z(shift):
        return (dp, lax.rem(z + shift + n_z, n_z) * PLANE + yc)

    def at_yc(shift):
        return (dp, z * PLANE + lax.rem(yc + shift, PLANE))

    def at_x(shift):
        return (lax.rem(dp + shift, n_dp), z * PLANE + yc)

    half = n_z // 2
    greet(
        [at_z(1), at_z(-1), at_z(half)]
        + [at_yc(i) for i in range(1, PLANE)]
        + [at_x(i) for i in range(1, 4)]
    )

    hops = [(k - 1, k, -1) for k in range(1, 5)] + [(1 - k, -k, 1) for k in range(1, 4)]

    def hop(buf, first, send, recv, number):
        here, there, way = hops[number]
        g, b = PLACE[there]
        source = first if here == 0 else buf.at[PLACE[here][0], PLACE[here][1]]
        return remote(source, buf.at[g, b], send.at[number], recv.at[number], at_z(way))

    t_hop = functools.partial(hop, xt, tokens, t_send, t_recv)
    c_hop = functools.partial(hop, xc, cot, c_send, c_recv)
    r_hop = functools.partial(hop, rg, rg.at[0, 0], r_send, r_recv)

    t_hop(0).start()
    t_hop(4).start()

    n_slots, count = rg.shape[2] // 2, rg.shape[3]
    row = lax.broadcasted_iota(jnp.int32, (n_slots, count), 0)
    col = lax.broadcasted_iota(jnp.int32, (n_slots, count), 1)
    named = jnp.zeros((n_slots, count), f32)
    weight = jnp.zeros((n_slots, count), f32)
    for k in range(routes_t.shape[0]):
        hit = routes_t[k : k + 1, :] == row
        named = named + jnp.where(hit, 1.0, 0.0)
        weight = weight + jnp.where(hit, gates_t[k : k + 1, :], 0.0)
    to_slot = jnp.where(partner[...] == col, 1.0, 0.0).astype(bf16)
    named = dot_nn(to_slot, named.astype(bf16))
    weight = dot_nn(to_slot, weight.astype(bf16))
    upto = jnp.where(row <= col, 1.0, 0.0).astype(bf16)
    rank = named * dot_nn(named.astype(bf16), upto)
    rg[0, 0, :n_slots, :] = rank.astype(bf16)
    rg[0, 0, n_slots:, :] = weight.astype(bf16)
    r_hop(0).start()
    r_hop(4).start()
    xt[0, 0] = tokens[...]
    xc[0, 0] = cot[...]

    per_plane = n_slots // n_z

    def build(g):
        for b in range(BLOCKS):
            start = pl.multiple_of(z * per_plane, per_plane)
            ranks = rg[g, b, pl.ds(start, per_plane), :]
            gates = rg[g, b, pl.ds(n_slots + start, per_plane), :]
            hit = dot_nn(expand[...], ranks) == wanted[:, b : b + 1]
            spread = dot_nn(expand[...], gates)
            columns = slice(b * count, (b + 1) * count)
            pick[g, :, columns] = jnp.where(hit, 1.0, 0.0).astype(bf16)
            pick_gate[g, :, columns] = jnp.where(hit, spread, 0.0).astype(bf16)

    width = tokens.shape[1]
    tile = 256

    def gather(matrix, buf, out, g):
        m = matrix[g]
        for j in range(width // tile):
            columns = pl.ds(j * tile, tile)
            block = buf[g, :, :, columns].reshape(BLOCKS * count, tile)
            out[g, :, :, columns] = dot_nn(m, block).astype(bf16).reshape(PLANE, 2 * ROWS, tile)

    def y_copy(out, got, phase, i):
        g = phase % 2
        p = lax.rem(yc + i, PLANE)
        return remote(out.at[g, p], got.at[g * PLANE + yc], y_send.at[phase, i], y_recv.at[phase, i], at_yc(i))

    def y_local(out, got, phase):
        g = phase % 2
        return pltpu.make_async_copy(out.at[g, yc], got.at[g * PLANE + yc], l_sem.at[phase])

    def y_start(out, got, phase):
        for i in range(1, PLANE):
            y_copy(out, got, phase, i).start()
        y_local(out, got, phase).start()

    def both(number, *makers):
        for make in makers:
            make(number).wait_recv()

    for k in (1, 2):
        both(k - 1, t_hop, r_hop)
        both(k + 3, t_hop, r_hop)
        t_hop(k).start()
        r_hop(k).start()
        t_hop(k + 4).start()
        r_hop(k + 4).start()
    build(0)
    gather(pick, xt, out_t, 0)
    y_start(out_t, got_t, 0)
    both(2, t_hop, r_hop)
    t_hop(3).start()
    r_hop(3).start()
    c_hop(0).start()
    c_hop(4).start()

    quarter = ws_gu.shape[0]
    rows = pl.ds(pl.multiple_of(dp * quarter, quarter), quarter)
    pairs = ((ws_gu, wr_gu), (ws_dn, wr_dn))

    def w_copy(n):
        return remote(pairs[n][0], pairs[n][1].at[rows, :], w_send.at[n], w_recv.at[n], at_z(half))

    def x_copy(n, i):
        here = pairs[n][1].at[rows, :]
        return remote(here, here, x_send.at[n, i], x_recv.at[n, i], at_x(i))

    w_copy(0).start()
    w_copy(1).start()
    both(6, t_hop, r_hop)
    both(3, t_hop, r_hop)
    build(1)
    gather(pick, xt, out_t, 1)
    both(0, c_hop)
    both(4, c_hop)
    c_hop(1).start()
    c_hop(5).start()
    y_start(out_t, got_t, 1)
    both(1, c_hop)
    both(5, c_hop)
    c_hop(2).start()
    c_hop(6).start()
    gather(pick_gate, xc, out_c, 0)
    y_start(out_c, got_c, 2)
    both(2, c_hop)
    c_hop(3).start()
    for n in range(2):
        w_copy(n).wait_recv()
        for i in range(1, 4):
            x_copy(n, i).start()
    both(6, c_hop)
    both(3, c_hop)
    gather(pick_gate, xc, out_c, 1)
    y_start(out_c, got_c, 3)

    for number in range(7):
        for make in (t_hop, c_hop, r_hop):
            make(number).wait_send()
    for phase in range(4):
        out, got = ((out_t, got_t), (out_c, got_c))[phase // 2]
        for i in range(1, PLANE):
            copy = y_copy(out, got, phase, i)
            copy.wait_send()
            copy.wait_recv()
        y_local(out, got, phase).wait()
    for n in range(2):
        w_copy(n).wait_send()
        for i in range(1, 4):
            x_copy(n, i).wait_send()
            x_copy(n, i).wait_recv()


def dispatch(tokens, routes, gates, cotangent, partner, ws_gu, ws_dn, n_slots, n_dp):
    count, width = tokens.shape
    n_z = lax.axis_size("expert") // PLANE
    per_plane = n_slots // n_z
    picked = per_plane * ROWS
    number = np.arange(picked)
    expand = (number[:, None] // ROWS == np.arange(per_plane)[None, :]).astype(np.float32)
    wanted = np.where(
        number[:, None] % ROWS // CAP == np.arange(BLOCKS)[None, :], (number % CAP + 1)[:, None], -1
    ).astype(np.float32)
    vmem, hbm = pl.BlockSpec(memory_space=pltpu.VMEM), pl.BlockSpec(memory_space=pl.ANY)
    dma = pltpu.SemaphoreType.DMA
    slab = jax.ShapeDtypeStruct((2 * PLANE, 2 * ROWS, width), bf16)
    matrix = jax.ShapeDtypeStruct((2, picked, BLOCKS * count), bf16)
    return pl.pallas_call(
        dispatch_kernel,
        out_shape=(
            slab, slab, matrix, matrix,
            jax.ShapeDtypeStruct((n_dp * ws_gu.shape[0], ws_gu.shape[1]), bf16),
            jax.ShapeDtypeStruct((n_dp * ws_dn.shape[0], ws_dn.shape[1]), bf16),
        ),
        in_specs=[vmem] * 7 + [hbm] * 2,
        out_specs=(hbm, hbm, vmem, vmem, hbm, hbm),
        scratch_shapes=[
            pltpu.VMEM((2, BLOCKS, count, width), bf16),
            pltpu.VMEM((2, BLOCKS, count, width), bf16),
            pltpu.VMEM((2, BLOCKS, 2 * n_slots, count), bf16),
            pltpu.VMEM((2, PLANE, 2 * ROWS, width), bf16),
            pltpu.VMEM((2, PLANE, 2 * ROWS, width), bf16),
            dma((7,)), dma((7,)), dma((7,)), dma((7,)), dma((7,)), dma((7,)),
            dma((4, PLANE)), dma((4, PLANE)), dma((4,)),
            dma((2,)), dma((2,)), dma((2, 4)), dma((2, 4)),
        ],
        compiler_params=pltpu.CompilerParams(
            collective_id=0, has_side_effects=True, vmem_limit_bytes=48 << 20
        ),
        name="dispatch",
    )(
        tokens, cotangent, routes.T, gates.T, partner[:, None],
        jnp.asarray(expand, bf16), jnp.asarray(wanted), ws_gu, ws_dn,
    )


def expert_kernel(
    moved, xt, xc, w_gu, w_dn, wr_gu, wr_dn, yo, yg, g_gu, g_dn, gu, dn, hid, gpre, sem
):
    j = pl.program_id(0)
    width = xt.shape[3]
    ff = hid.shape[1]
    chunks = PLANE
    rows = chunks * ROWS

    def load(gu_src, dn_src):
        a = pltpu.make_async_copy(gu_src, gu, sem.at[0])
        b = pltpu.make_async_copy(dn_src, dn, sem.at[1])
        a.start()
        b.start()
        a.wait()
        b.wait()

    @pl.when(moved[j] == 0)
    def _():
        load(w_gu.at[j], w_dn.at[j])

    @pl.when(moved[j] != 0)
    def _():
        load(wr_gu, wr_dn)

    @pl.loop(0, 2)
    def _(i):
        part = pl.ds(i * chunks, chunks)
        here = pl.ds(pl.multiple_of(i * rows, rows), rows)
        x = xt[part, 0].reshape(rows, width)
        pre = dot_nn(x, gu[...])
        gate, up = pre[:, :ff], pre[:, ff:]
        sig = jax.nn.sigmoid(gate)
        silu = gate * sig
        hidden = (silu * up).astype(bf16)
        hid[here, :] = hidden
        yo[part, 0] = dot_nt(hidden, dn[...]).astype(bf16).reshape(chunks, ROWS, width)
        c = xc[part, 0].reshape(rows, width)
        grad = dot_nn(c, dn[...])
        grad_gate = grad * up * sig * (1.0 + gate * (1.0 - sig))
        gpre[here, :ff] = grad_gate.astype(bf16)
        gpre[here, ff:] = (grad * silu).astype(bf16)
        yg[part, 0] = dot_nt(gpre[here, :], gu[...]).astype(bf16).reshape(chunks, ROWS, width)

    tile = 256

    @pl.loop(0, width // tile)
    def _(i):
        columns = pl.ds(pl.multiple_of(i * tile, tile), tile)
        x = xt[:, 0, :, columns].reshape(2 * rows, tile)
        g_gu[0, columns, :] = (dot_tn(x, gpre[...]) * grad_scale).astype(bf16)
        c = xc[:, 0, :, columns].reshape(2 * rows, tile)
        g_dn[0, columns, :] = (dot_tn(c, hid[...]) * grad_scale).astype(bf16)


def experts(moved, got_t, got_c, w_gu, w_dn, wr_gu, wr_dn):
    slots, width, ff2 = w_gu.shape
    ff = ff2 // 2
    shape = (2 * PLANE, slots, ROWS, width)
    hbm = pl.BlockSpec(memory_space=pl.ANY)
    slab = pl.BlockSpec((2 * PLANE, 1, ROWS, width), lambda j, m: (0, j, 0, 0))
    flat = (2 * PLANE, slots * ROWS, width)
    outs = pl.pallas_call(
        expert_kernel,
        grid_spec=pltpu.PrefetchScalarGridSpec(
            num_scalar_prefetch=1,
            grid=(slots,),
            in_specs=[slab, slab, hbm, hbm, hbm, hbm],
            out_specs=(
                slab,
                slab,
                pl.BlockSpec((1, width, ff2), lambda j, m: (j, 0, 0)),
                pl.BlockSpec((1, width, ff), lambda j, m: (j, 0, 0)),
            ),
            scratch_shapes=[
                pltpu.VMEM((width, ff2), bf16),
                pltpu.VMEM((width, ff), bf16),
                pltpu.VMEM((2 * PLANE * ROWS, ff), bf16),
                pltpu.VMEM((2 * PLANE * ROWS, ff2), bf16),
                pltpu.SemaphoreType.DMA((2,)),
            ],
        ),
        out_shape=(
            jax.ShapeDtypeStruct(shape, bf16),
            jax.ShapeDtypeStruct(shape, bf16),
            jax.ShapeDtypeStruct((slots, width, ff2), bf16),
            jax.ShapeDtypeStruct((slots, width, ff), bf16),
        ),
        compiler_params=pltpu.CompilerParams(vmem_limit_bytes=56 << 20),
        name="experts",
    )(moved, got_t.reshape(shape), got_c.reshape(shape), w_gu, w_dn, wr_gu, wr_dn)
    return outs[0].reshape(flat), outs[1].reshape(flat), outs[2], outs[3]


def combine_kernel(
    yo, yg, pick, pick_gate, g_gu, g_dn,
    mixed, grad_tokens, xr_gu, xr_dn,
    ybuf, part, ring_in, ring_out,
    y_send, y_recv, l_sem, z_send, z_recv, x_send, x_recv,
):
    dp, z, yc, n_dp, n_z = places()

    def at_z(shift):
        return (dp, lax.rem(z + shift + n_z, n_z) * PLANE + yc)

    def at_yc(shift):
        return (dp, z * PLANE + lax.rem(yc + shift, PLANE))

    def at_x(shift):
        return (lax.rem(dp + shift, n_dp), z * PLANE + yc)

    greet(
        [at_z(1), at_z(-1)]
        + [at_yc(i) for i in range(1, PLANE)]
        + [at_x(i) for i in range(1, 4)]
    )

    def y_copy(phase, i):
        source, g = (yo, yg)[phase // 2], 1 - phase % 2
        p = lax.rem(yc + i, PLANE)
        return remote(
            source.at[g * PLANE + p], ybuf.at[phase, yc], y_send.at[phase, i], y_recv.at[phase, i], at_yc(i)
        )

    def y_local(phase):
        source, g = (yo, yg)[phase // 2], 1 - phase % 2
        return pltpu.make_async_copy(source.at[g * PLANE + yc], ybuf.at[phase, yc], l_sem.at[phase])

    def y_start(phase):
        for i in range(1, PLANE):
            y_copy(phase, i).start()
        y_local(phase).start()

    quarter = xr_gu.shape[2]
    pairs = ((g_gu, xr_gu), (g_dn, xr_dn))

    def x_copy(n, i):
        to = lax.rem(dp + i, n_dp)
        rows = pl.ds(pl.multiple_of(to * quarter, quarter), quarter)
        return remote(
            pairs[n][0].at[:, rows, :], pairs[n][1].at[i - 1], x_send.at[n, i], x_recv.at[n, i], at_x(i)
        )

    y_start(0)
    for n in range(2):
        for i in range(1, 4):
            x_copy(n, i).start()
    y_start(1)

    count, width = mixed.shape
    tile = 256

    def y_take(phase):
        for i in range(1, PLANE):
            y_copy(phase, i).wait_recv()
        y_local(phase).wait()
        stream, g = phase // 2, 1 - phase % 2
        matrix = (pick_gate, pick)[stream]
        for j in range(width // tile):
            columns = pl.ds(j * tile, tile)
            y = ybuf[phase, :, :, columns].reshape(PLANE * 2 * ROWS, tile)
            part[g, :, columns] = dot_tn(matrix[g], y)

    def own(offset):
        g, b = PLACE[offset]
        return part[g, b * count : (b + 1) * count, :]

    offsets = (3, 2, 1, 4, -3, -2, -1)

    def z_copy(stream, n):
        way = 1 if n < 3 else -1
        return remote(
            ring_out.at[stream, n], ring_in.at[stream, n], z_send.at[stream, n], z_recv.at[stream, n], at_z(way)
        )

    def z_step(stream, n):
        total = own(offsets[n])
        if n not in (0, 3):
            z_copy(stream, n - 1).wait_recv()
            total = total + ring_in[stream, n - 1].astype(f32)
        ring_out[stream, n] = total.astype(bf16)
        z_copy(stream, n).start()

    for stream in range(2):
        y_take(2 * stream)
        z_step(stream, 0)
        z_step(stream, 3)
        if stream == 0:
            y_start(2)
        z_step(stream, 1)
        z_step(stream, 4)
        y_take(2 * stream + 1)
        z_step(stream, 2)
        z_step(stream, 5)
        if stream == 0:
            y_start(3)
        z_step(stream, 6)
        z_copy(stream, 2).wait_recv()
        z_copy(stream, 6).wait_recv()
        total = own(0) + ring_in[stream, 2].astype(f32) + ring_in[stream, 6].astype(f32)
        (mixed, grad_tokens)[stream][...] = total.astype(bf16)

    for stream in range(2):
        for n in range(7):
            z_copy(stream, n).wait_send()
    for phase in range(4):
        for i in range(1, PLANE):
            y_copy(phase, i).wait_send()
    for n in range(2):
        for i in range(1, 4):
            x_copy(n, i).wait_send()
            x_copy(n, i).wait_recv()


def combine(yo, yg, pick, pick_gate, g_gu, g_dn, count, n_dp):
    slots, width, ff2 = g_gu.shape
    ff = ff2 // 2
    quarter = width // n_dp
    vmem, hbm = pl.BlockSpec(memory_space=pltpu.VMEM), pl.BlockSpec(memory_space=pl.ANY)
    dma = pltpu.SemaphoreType.DMA
    own = jax.ShapeDtypeStruct((count, width), bf16)
    return pl.pallas_call(
        combine_kernel,
        out_shape=(
            own, own,
            jax.ShapeDtypeStruct((n_dp - 1, slots, quarter, ff2), bf16),
            jax.ShapeDtypeStruct((n_dp - 1, slots, quarter, ff), bf16),
        ),
        in_specs=[hbm, hbm, vmem, vmem, hbm, hbm],
        out_specs=(vmem, vmem, hbm, hbm),
        scratch_shapes=[
            pltpu.VMEM((4, PLANE, 2 * ROWS, width), bf16),
            pltpu.VMEM((2, BLOCKS * count, width), f32),
            pltpu.VMEM((2, 7, count, width), bf16),
            pltpu.VMEM((2, 7, count, width), bf16),
            dma((4, PLANE)), dma((4, PLANE)), dma((4,)), dma((2, 7)), dma((2, 7)), dma((2, 4)), dma((2, 4)),
        ],
        compiler_params=pltpu.CompilerParams(
            collective_id=1, has_side_effects=True, vmem_limit_bytes=48 << 20
        ),
        name="combine",
    )(yo, yg, pick, pick_gate, g_gu, g_dn)


def local(tokens, routes, gates, cotangent, partner, w_gate_up, w_down):
    slots, width, ff2 = w_gate_up.shape
    n_dp, n_expert = lax.axis_size("dp"), lax.axis_size("expert")
    dp, index = lax.axis_index("dp"), lax.axis_index("expert")
    quarter = width // n_dp
    mine = lax.dynamic_slice(partner, (index * slots,), (slots,))
    moved = (mine // slots != index).astype(jnp.int32)
    going = jnp.argmax(moved).astype(jnp.int32)
    ws_gu = lax.dynamic_slice(w_gate_up, (going, dp * quarter, 0), (1, quarter, ff2))[0]
    ws_dn = lax.dynamic_slice(w_down, (going, dp * quarter, 0), (1, quarter, ff2 // 2))[0]
    got_t, got_c, pick, pick_gate, wr_gu, wr_dn = dispatch(
        tokens, routes, gates, cotangent, partner, ws_gu, ws_dn, n_expert * slots, n_dp
    )
    yo, yg, g_gu, g_dn = experts(moved, got_t, got_c, w_gate_up, w_down, wr_gu, wr_dn)
    mixed, grad_tokens, xr_gu, xr_dn = combine(
        yo, yg, pick, pick_gate, g_gu, g_dn, tokens.shape[0], n_dp
    )

    def total(own, others):
        own = lax.dynamic_slice(own, (0, dp * quarter, 0), (slots, quarter, own.shape[2]))
        return own.astype(f32) + jnp.sum(others.astype(f32), axis=0)

    return mixed, grad_tokens, total(g_gu, xr_gu), total(g_dn, xr_dn)


def solution(mesh):
    token_spec = P(("dp", "expert"), None)
    weight_spec = P("expert", None, None)
    grad_spec = P("expert", "dp", None)
    return jax.shard_map(
        local,
        mesh=mesh,
        in_specs=(token_spec, token_spec, token_spec, token_spec, P(None), weight_spec, weight_spec),
        out_specs=(token_spec, token_spec, grad_spec, grad_spec),
        check_vma=False,
    )
```

```python
import jax
import jax.numpy as jnp
from jax import lax
from jax.experimental import pallas as pl
from jax.experimental.pallas import tpu as pltpu
from jax.sharding import PartitionSpec as P

MESH = pl.DeviceIdType.MESH
bf16, f32 = jnp.bfloat16, jnp.float32

grad_scale = 0.0625
PLANE = 8
CAP = 12
BLOCKS = 4
ROWS = CAP * BLOCKS
SLOTS = 2
GROUPS = ((0, 1, -1, -2), (2, 3, -3, 4))
PLACE = {offset: g * BLOCKS + b for g, group in enumerate(GROUPS) for b, offset in enumerate(group)}
HOPS = [(k - 1, k, -1) for k in range(1, 5)] + [(1 - k, -k, 1) for k in range(1, 4)]
BACK = (3, 2, 1, 4, -3, -2, -1)
TILE = 256


def dot_nn(a, b):
    return lax.dot_general(a, b, (((1,), (0,)), ((), ())), preferred_element_type=f32)


def dot_nt(a, b):
    return lax.dot_general(a, b, (((1,), (1,)), ((), ())), preferred_element_type=f32)


def dot_tn(a, b):
    return lax.dot_general(a, b, (((0,), (0,)), ((), ())), preferred_element_type=f32)


def remote(src, dst, send, recv, device):
    return pltpu.make_async_remote_copy(
        src_ref=src, dst_ref=dst, send_sem=send, recv_sem=recv, device_id=device, device_id_type=MESH
    )


def layer_kernel(
    tokens, routes_t, gates_t, cot, partner, w_gu, w_dn,
    mixed, grad_tokens, own_gu, own_dn, xr_gu, xr_dn,
    tok_v, cot_v, routes_v, gates_v, partner_v,
    xt, xc, rg, pick, pick_gate, out_t, out_c, got_t, got_c,
    gu, dn, ws_gu, ws_dn, wr_gu, wr_dn,
    pre, hid, gpre, g_gu, g_dn, ybuf, part, ring_in,
    load_sem, t_send, t_recv, r_send, r_recv, y_send, y_recv, l_sem, w_send, w_recv, v_send, v_recv,
    b_send, b_recv, bl_sem, z_send, z_recv, x_send, x_recv, own_sem,
):
    dp, index = lax.axis_index("dp"), lax.axis_index("expert")
    n_dp, n_z = lax.axis_size("dp"), lax.axis_size("expert") // PLANE
    z, yc = index // PLANE, index % PLANE
    count, width = tokens.shape
    half = width // 2
    ff = dn.shape[2]
    n_slots = lax.axis_size("expert") * SLOTS
    picked = PLANE * SLOTS * ROWS
    quarter = width // n_dp

    def at_z(shift):
        return (dp, lax.rem(z + shift + n_z, n_z) * PLANE + yc)

    def at_yc(shift):
        return (dp, z * PLANE + lax.rem(yc + shift, PLANE))

    def at_x(shift):
        return (lax.rem(dp + shift, n_dp), z * PLANE + yc)

    loads = [
        pltpu.make_async_copy(src, dst, load_sem.at[n])
        for n, (src, dst) in enumerate(
            (
                (tokens, tok_v), (routes_t, routes_v), (gates_t, gates_v), (partner, partner_v),
                (cot, cot_v), (w_gu, gu), (w_dn, dn),
            )
        )
    ]
    for load in loads:
        load.start()

    barrier = pltpu.get_barrier_semaphore()
    peers = [at_z(1), at_z(-1), at_z(n_z // 2)]
    peers += [at_yc(i) for i in range(1, PLANE)] + [at_x(i) for i in range(1, 4)]
    for device in peers:
        pl.semaphore_signal(barrier, inc=1, device_id=device, device_id_type=MESH)
    pl.semaphore_wait(barrier, len(peers))

    def rows_of(s):
        return (xt, xc)[s // 2].at[s % 2]

    def hop(s, n):
        here, there, way = HOPS[n]
        buf = rows_of(s)
        return remote(buf.at[PLACE[here]], buf.at[PLACE[there]], t_send.at[s, n], t_recv.at[s, n], at_z(way))

    def r_hop(n):
        here, there, way = HOPS[n]
        return remote(rg.at[PLACE[here]], rg.at[PLACE[there]], r_send.at[n], r_recv.at[n], at_z(way))

    for n in range(4):
        loads[n].wait()
    for h in range(2):
        xt[h, 0] = tok_v[:, h * half : (h + 1) * half]
        hop(h, 0).start()
        hop(h, 4).start()

    row = lax.broadcasted_iota(jnp.int32, (n_slots, count), 0)
    col = lax.broadcasted_iota(jnp.int32, (n_slots, count), 1)
    named = jnp.zeros((n_slots, count), f32)
    weight = jnp.zeros((n_slots, count), f32)
    for k in range(routes_t.shape[0]):
        hit = routes_v[k : k + 1, :] == row
        named = named + jnp.where(hit, 1.0, 0.0)
        weight = weight + jnp.where(hit, gates_v[k : k + 1, :], 0.0)
    to_slot = jnp.where(partner_v[...] == row, 1.0, 0.0).astype(bf16)
    named = dot_tn(to_slot, named.astype(bf16))
    weight = dot_tn(to_slot, weight.astype(bf16))
    upto = jnp.where(row <= col, 1.0, 0.0).astype(bf16)
    rank = named * dot_nn(named.astype(bf16), upto)
    rg[0, :n_slots, :] = rank.astype(bf16)
    rg[0, n_slots:, :] = weight.astype(bf16)
    r_hop(0).start()
    r_hop(4).start()

    lane = lax.broadcasted_iota(jnp.int32, (1, n_slots), 1)
    moved = []
    for j in range(SLOTS):
        held = jnp.where(lane == index * SLOTS + j, partner_v[...], 0)
        held = jnp.sum(held.astype(f32), axis=1, keepdims=True)
        first = (index * SLOTS).astype(f32)
        moved.append((held < first) | (held > first + (SLOTS - 1)))

    loads[4].wait()
    for h in range(2):
        xc[h, 0] = cot_v[:, h * half : (h + 1) * half]
    loads[5].wait()
    loads[6].wait()
    mine = pl.ds(pl.multiple_of(dp * quarter, quarter), quarter)
    ws_gu[...] = jnp.where(moved[1], gu[1, mine, :], gu[0, mine, :])
    ws_dn[...] = jnp.where(moved[1], dn[1, mine, :], dn[0, mine, :])

    number = lax.broadcasted_iota(jnp.int32, (picked, 1), 0).astype(f32)
    slot_of = jnp.floor((number + 0.5) * (1.0 / ROWS))
    rest = number - ROWS * slot_of
    block_of = jnp.floor((rest + 0.5) * (1.0 / CAP))
    rank_of = rest - CAP * block_of + 1.0
    per_plane = PLANE * SLOTS
    slot_lane = lax.broadcasted_iota(jnp.int32, (picked, per_plane), 1).astype(f32)
    expand = jnp.where(slot_lane == slot_of, 1.0, 0.0).astype(bf16)

    def build(g):
        for b in range(BLOCKS):
            start = pl.multiple_of(z * per_plane, per_plane)
            ranks = rg[g * BLOCKS + b, pl.ds(start, per_plane), :]
            gates = rg[g * BLOCKS + b, pl.ds(n_slots + start, per_plane), :]
            hit = dot_nn(expand, ranks) == jnp.where(block_of == b, rank_of, -1.0)
            spread = dot_nn(expand, gates)
            columns = slice(b * count, (b + 1) * count)
            pick[g, :, columns] = jnp.where(hit, 1.0, 0.0).astype(bf16)
            pick_gate[g, :, columns] = jnp.where(hit, spread, 0.0).astype(bf16)

    def out_of(s):
        return (out_t, out_c)[s // 2]

    def got_of(s):
        return (got_t, got_c)[s // 2]

    def y_copy(s, g, i):
        p = lax.rem(yc + i, PLANE)
        n = 2 * s + g
        return remote(
            out_of(s).at[s % 2, g, p], got_of(s).at[s % 2, g, yc], y_send.at[n, i], y_recv.at[n, i], at_yc(i)
        )

    def y_local(s, g):
        return pltpu.make_async_copy(
            out_of(s).at[s % 2, g, yc], got_of(s).at[s % 2, g, yc], l_sem.at[2 * s + g]
        )

    def send_rows(s, g):
        matrix, buf, out = (pick, pick_gate)[s // 2], (xt, xc)[s // 2], out_of(s)

        @pl.loop(0, half // TILE)
        def _(j):
            columns = pl.ds(pl.multiple_of(j * TILE, TILE), TILE)
            block = buf[s % 2, g * BLOCKS : (g + 1) * BLOCKS, :, columns].reshape(BLOCKS * count, TILE)
            rows = dot_nn(matrix[g], block).astype(bf16)
            out[s % 2, g, :, :, columns] = rows.reshape(PLANE, SLOTS * ROWS, TILE)

        for i in range(1, PLANE):
            y_copy(s, g, i).start()
        y_local(s, g).start()

    def rows_arrived(s, g):
        for i in range(1, PLANE):
            y_copy(s, g, i).wait_recv()
        y_local(s, g).wait()

    def rows_left(s, g):
        for i in range(1, PLANE):
            y_copy(s, g, i).wait_send()

    def ring(s, k, follow=True):
        hop(s, k - 1).wait_recv()
        if k < 4:
            hop(s, k + 3).wait_recv()
        if k < 4:
            hop(s, k).start()
        if k < 3:
            hop(s, k + 4).start()

    def r_ring(k):
        r_hop(k - 1).wait_recv()
        if k < 4:
            r_hop(k + 3).wait_recv()
            r_hop(k).start()
        if k < 3:
            r_hop(k + 4).start()

    traded = ((ws_gu, wr_gu), (ws_dn, wr_dn))

    def w_copy(n):
        return remote(traded[n][0], traded[n][1].at[mine, :], w_send.at[n], w_recv.at[n], at_z(n_z // 2))

    def v_copy(n, i):
        here = traded[n][1].at[mine, :]
        return remote(here, here, v_send.at[n, i], v_recv.at[n, i], at_x(i))

    ring(0, 1)
    r_ring(1)
    ring(1, 1)
    ring(0, 2)
    r_ring(2)
    build(0)
    send_rows(0, 0)
    ring(1, 2)
    send_rows(1, 0)
    ring(0, 3)
    r_ring(3)
    ring(1, 3)
    for s in (2, 3):
        hop(s, 0).start()
        hop(s, 4).start()
    w_copy(0).start()
    w_copy(1).start()
    ring(0, 4)
    r_ring(4)
    build(1)
    send_rows(0, 1)
    ring(1, 4)
    send_rows(1, 1)
    ring(2, 1)
    ring(3, 1)
    ring(2, 2)
    ring(3, 2)
    send_rows(2, 0)
    send_rows(3, 0)
    ring(2, 3)
    ring(3, 3)
    ring(2, 4)
    send_rows(2, 1)
    ring(3, 4)
    send_rows(3, 1)
    for n in range(2):
        w_copy(n).wait_recv()
        for i in range(1, 4):
            v_copy(n, i).start()
    for n in range(2):
        for i in range(1, 4):
            v_copy(n, i).wait_recv()

    @pl.loop(0, width // TILE)
    def _(i):
        rows = pl.ds(pl.multiple_of(i * TILE, TILE), TILE)
        for j in range(SLOTS):
            gu[j, rows, :] = jnp.where(moved[j], wr_gu[rows, :], gu[j, rows, :])
            dn[j, rows, :] = jnp.where(moved[j], wr_dn[rows, :], dn[j, rows, :])

    many = PLANE * ROWS

    def b_copy(s, g, i):
        p = lax.rem(yc + i, PLANE)
        n = 2 * s + g
        return remote(
            out_of(s).at[s % 2, g, p], ybuf.at[n, yc], b_send.at[n, i], b_recv.at[n, i], at_yc(i)
        )

    def b_local(s, g):
        return pltpu.make_async_copy(out_of(s).at[s % 2, g, yc], ybuf.at[2 * s + g, yc], bl_sem.at[2 * s + g])

    def b_start(s, g):
        for i in range(1, PLANE):
            b_copy(s, g, i).start()
        b_local(s, g).start()

    def slot_rows(buf, h, g, j):
        return buf[h, g, :, j * ROWS : (j + 1) * ROWS, :].reshape(many, half)

    def put_rows(buf, h, g, j, value):
        buf[h, g, :, j * ROWS : (j + 1) * ROWS, :] = value.astype(bf16).reshape(PLANE, ROWS, half)

    for s in range(2):
        for g in range(2):
            rows_arrived(s, g)
            rows_left(s, g)
    for g in (1, 0):
        for j in range(SLOTS):
            x = slot_rows(got_t, 0, g, j)
            first = dot_nn(x, gu[j, :half, :])
            x = slot_rows(got_t, 1, g, j)
            both = first + dot_nn(x, gu[j, half:, :])
            pre[j, g] = both
            gate, up = both[:, :ff], both[:, ff:]
            hidden = (gate * jax.nn.sigmoid(gate) * up).astype(bf16)
            hid[j, g] = hidden
            for h in range(2):
                put_rows(out_t, h, g, j, dot_nt(hidden, dn[j, h * half : (h + 1) * half, :]))
        for s in range(2):
            b_start(s, g)

    for g in (0, 1):
        for s in (2, 3):
            rows_arrived(s, g)
            rows_left(s, g)
        for j in range(SLOTS):
            c = slot_rows(got_c, 0, g, j)
            first = dot_nn(c, dn[j, :half, :])
            c = slot_rows(got_c, 1, g, j)
            grad = first + dot_nn(c, dn[j, half:, :])
            gate, up = pre[j, g, :, :ff], pre[j, g, :, ff:]
            sig = jax.nn.sigmoid(gate)
            gpre[j, g, :, :ff] = (grad * up * sig * (1.0 + gate * (1.0 - sig))).astype(bf16)
            gpre[j, g, :, ff:] = (grad * (gate * sig)).astype(bf16)
            for h in range(2):
                put_rows(out_c, h, g, j, dot_nt(gpre[j, g], gu[j, h * half : (h + 1) * half, :]))
    for g in (1, 0):
        for s in (2, 3):
            b_start(s, g)

    for j in range(SLOTS):
        for h in range(2):

            @pl.loop(0, half // TILE)
            def _(i):
                columns = pl.ds(pl.multiple_of(i * TILE, TILE), TILE)
                to = pl.ds(pl.multiple_of(h * half + i * TILE, TILE), TILE)
                block = slice(j * ROWS, (j + 1) * ROWS)
                x = got_t[h, :, :, block, columns].reshape(2 * many, TILE)
                g_gu[j, to, :] = (dot_tn(x, gpre[j].reshape(2 * many, 2 * ff)) * grad_scale).astype(bf16)
                c = got_c[h, :, :, block, columns].reshape(2 * many, TILE)
                g_dn[j, to, :] = (dot_tn(c, hid[j].reshape(2 * many, ff)) * grad_scale).astype(bf16)

    grads = ((g_gu, xr_gu, own_gu), (g_dn, xr_dn, own_dn))

    def x_copy(n, i):
        to = lax.rem(dp + i, n_dp)
        rows = pl.ds(pl.multiple_of(to * quarter, quarter), quarter)
        return remote(
            grads[n][0].at[:, rows, :], grads[n][1].at[i - 1], x_send.at[n, i], x_recv.at[n, i], at_x(i)
        )

    def own_copy(n):
        return pltpu.make_async_copy(grads[n][0].at[:, mine, :], grads[n][2], own_sem.at[n])

    for n in range(2):
        for i in range(1, 4):
            x_copy(n, i).start()
        own_copy(n).start()

    for s in range(4):
        for n in range(7):
            hop(s, n).wait_send()

    def combine(s, g):
        for i in range(1, PLANE):
            b_copy(s, g, i).wait_recv()
        b_local(s, g).wait()
        matrix = (pick_gate, pick)[s // 2]

        @pl.loop(0, half // TILE)
        def _(j):
            columns = pl.ds(pl.multiple_of(j * TILE, TILE), TILE)
            y = ybuf[2 * s + g, :, :, columns].reshape(picked, TILE)
            part[s % 2, g, :, columns] = dot_tn(matrix[g], y)

    def own_part(s, offset):
        g, b = PLACE[offset] // BLOCKS, PLACE[offset] % BLOCKS
        return part[s % 2, g, b * count : (b + 1) * count, :]

    def z_copy(s, n):
        way = 1 if n < 3 else -1
        return remote(rows_of(s).at[n], ring_in.at[s, n], z_send.at[s, n], z_recv.at[s, n], at_z(way))

    def z_step(s, n):
        total = own_part(s, BACK[n])
        if n not in (0, 3):
            z_copy(s, n - 1).wait_recv()
            total = total + ring_in[s, n - 1].astype(f32)
        rows_of(s)[n] = total.astype(bf16)
        z_copy(s, n).start()

    def finish(s):
        z_copy(s, 2).wait_recv()
        z_copy(s, 6).wait_recv()
        total = own_part(s, 0) + ring_in[s, 2].astype(f32) + ring_in[s, 6].astype(f32)
        to = slice(s % 2 * half, (s % 2 + 1) * half)
        (mixed, grad_tokens)[s // 2][:, to] = total.astype(bf16)

    for pair in ((0, 1), (2, 3)):
        for s in pair:
            combine(s, 1)
            z_step(s, 0)
            z_step(s, 3)
        for s in pair:
            z_step(s, 1)
            z_step(s, 4)
        for s in pair:
            combine(s, 0)
            z_step(s, 2)
            z_step(s, 5)
        for s in pair:
            z_step(s, 6)
        for s in pair:
            finish(s)

    for n in range(7):
        r_hop(n).wait_send()
        for s in range(4):
            z_copy(s, n).wait_send()
    for s in range(4):
        for g in range(2):
            for i in range(1, PLANE):
                b_copy(s, g, i).wait_send()
    for n in range(2):
        w_copy(n).wait_send()
        own_copy(n).wait()
        for i in range(1, 4):
            v_copy(n, i).wait_send()
            x_copy(n, i).wait_send()
            x_copy(n, i).wait_recv()


def layer(tokens, routes, gates, cotangent, partner, w_gu, w_dn):
    count, width = tokens.shape
    slots, _, ff2 = w_gu.shape
    ff, half = ff2 // 2, width // 2
    n_dp, n_slots = lax.axis_size("dp"), lax.axis_size("expert") * slots
    quarter = width // n_dp
    picked = PLANE * SLOTS * ROWS
    vmem, hbm = pl.BlockSpec(memory_space=pltpu.VMEM), pl.BlockSpec(memory_space=pl.ANY)
    dma = pltpu.SemaphoreType.DMA
    many = PLANE * ROWS
    shape = jax.ShapeDtypeStruct
    return pl.pallas_call(
        layer_kernel,
        out_shape=(
            shape((count, width), bf16), shape((count, width), bf16),
            shape((slots, quarter, ff2), bf16), shape((slots, quarter, ff), bf16),
            shape((n_dp - 1, slots, quarter, ff2), bf16), shape((n_dp - 1, slots, quarter, ff), bf16),
        ),
        in_specs=[hbm] * 7,
        out_specs=(vmem, vmem, hbm, hbm, hbm, hbm),
        scratch_shapes=[
            pltpu.VMEM((count, width), bf16), pltpu.VMEM((count, width), bf16),
            pltpu.VMEM(routes.shape[::-1], jnp.int32), pltpu.VMEM(gates.shape[::-1], f32),
            pltpu.VMEM((1, n_slots), jnp.int32),
            pltpu.VMEM((2, 2 * BLOCKS, count, half), bf16), pltpu.VMEM((2, 2 * BLOCKS, count, half), bf16),
            pltpu.VMEM((2 * BLOCKS, 2 * n_slots, count), bf16),
            pltpu.VMEM((2, picked, BLOCKS * count), bf16), pltpu.VMEM((2, picked, BLOCKS * count), bf16),
            pltpu.VMEM((2, 2, PLANE, SLOTS * ROWS, half), bf16),
            pltpu.VMEM((2, 2, PLANE, SLOTS * ROWS, half), bf16),
            pltpu.VMEM((2, 2, PLANE, SLOTS * ROWS, half), bf16),
            pltpu.VMEM((2, 2, PLANE, SLOTS * ROWS, half), bf16),
            pltpu.VMEM((slots, width, ff2), bf16), pltpu.VMEM((slots, width, ff), bf16),
            pltpu.VMEM((quarter, ff2), bf16), pltpu.VMEM((quarter, ff), bf16),
            pltpu.VMEM((width, ff2), bf16), pltpu.VMEM((width, ff), bf16),
            pltpu.VMEM((slots, 2, many, ff2), f32),
            pltpu.VMEM((slots, 2, many, ff), bf16), pltpu.VMEM((slots, 2, many, ff2), bf16),
            pltpu.VMEM((slots, width, ff2), bf16), pltpu.VMEM((slots, width, ff), bf16),
            pltpu.VMEM((8, PLANE, SLOTS * ROWS, half), bf16),
            pltpu.VMEM((2, 2, BLOCKS * count, half), f32),
            pltpu.VMEM((4, 7, count, half), bf16),
            dma((7,)), dma((4, 7)), dma((4, 7)), dma((7,)), dma((7,)),
            dma((8, PLANE)), dma((8, PLANE)), dma((8,)), dma((2,)), dma((2,)), dma((2, 4)), dma((2, 4)),
            dma((8, PLANE)), dma((8, PLANE)), dma((8,)), dma((4, 7)), dma((4, 7)), dma((2, 4)), dma((2, 4)),
            dma((2,)),
        ],
        compiler_params=pltpu.CompilerParams(
            collective_id=0, has_side_effects=True, vmem_limit_bytes=62 << 20
        ),
        name="layer",
    )(tokens, routes.T, gates.T, cotangent, partner[None, :], w_gu, w_dn)


def local(*args):
    mixed, grad_tokens, own_gu, own_dn, xr_gu, xr_dn = layer(*args)

    def total(own, others):
        return own.astype(f32) + jnp.sum(others.astype(f32), axis=0)

    return mixed, grad_tokens, total(own_gu, xr_gu), total(own_dn, xr_dn)


def solution(mesh):
    token_spec = P(("dp", "expert"), None)
    weight_spec = P("expert", None, None)
    grad_spec = P("expert", "dp", None)
    return jax.shard_map(
        local,
        mesh=mesh,
        in_specs=(token_spec, token_spec, token_spec, token_spec, P(None), weight_spec, weight_spec),
        out_specs=(token_spec, token_spec, grad_spec, grad_spec),
        check_vma=False,
    )
```
